256 devices in a mesh: br: 8 (over y_lo, x), bus: 32 (over y_hi, z, core).
Axes of the slice: x: 4, y: 4 (y_hi: 2, y_lo: 2; y = y_hi * 2 + y_lo), z: 8, core: 2. Of those that a mesh axis runs over, the one named last changes fastest.
Arguments:
- ptdf: bfloat16 [8192, 65536], P('br', 'bus'), may hold values from -0.0234375 to 0.0234375
- load_codes: int32 [65536, 1024], P('bus'), may hold values from -4096 to 4096
- limit_codes: int32 [8192], P('br'), may hold values from 64 to 320
Outputs:
- penalty: float32 [8192, 1024], P(('br', 'bus'))
- sensitivity: float32 [65536, 1024], P('bus', 'br')
The draws below stay inside these ranges and needn't reach their ends.
All inputs are finite; a program needn't handle non-finite values.
Results may differ from the reference program's by a relative error of at most 0.004.
Values may be sent and summed in bfloat16 or wider, within the bound.
A program may use at most 128 MiB of HBM per device.

```python
import jax
import jax.numpy as jnp
from jax import lax

NB = 65536
BR = 8192
HOURS = 1024


def with_ends(drawn, stream_key, smallest, largest):
    longest = drawn.shape.index(max(drawn.shape))
    spots = []
    for shift in (0, 1):
        where = [jax.random.randint(jax.random.fold_in(stream_key, axis), (), 0, length) for axis, length in enumerate(drawn.shape)]
        where[longest] = (where[longest] + shift) % drawn.shape[longest]
        spots.append(tuple(where))
    return drawn.at[spots[0]].set(smallest).at[spots[1]].set(largest)


def steps_of(key, shape, split, least, high):
    factor_of = 1.0
    for axis_at, parts in split:
        heights = jax.random.uniform(jax.random.fold_in(jax.random.fold_in(key, 6), axis_at), (parts,), jnp.float32, least / len(split), high / len(split))
        factor_of = factor_of * jnp.repeat(jnp.exp(heights), shape[axis_at] // parts).reshape((-1,) + (1,) * (len(shape) - 1 - axis_at))
    return factor_of


def bell_draw(own_key, shape, deviation, limit, cuts=(), kind=jnp.bfloat16):
    array = deviation * jax.random.normal(own_key, shape, jnp.float32)
    if cuts:
        array = array * steps_of(own_key, shape, cuts, -0.22, 0.18)
    return jnp.clip(array, -limit, limit).astype(kind)


def setup_inputs(seed: int = 0) -> dict:
    streams_of = jax.random.split(jax.random.key(seed), 4)
    return {
        "ptdf": bell_draw(streams_of[0], (BR, NB), NB ** -0.5, 0.0234375, ((0, 8), (1, 32))),
        "load_codes": with_ends(jax.random.randint(streams_of[1], (NB, HOURS), -4096, 4097), jax.random.fold_in(streams_of[1], 1), -4096, 4096).astype(jnp.int32),
        "limit_codes": with_ends(jax.random.randint(streams_of[2], (BR,), 64, 321), jax.random.fold_in(streams_of[2], 1), 64, 320).astype(jnp.int32),
    }


def reference(ptdf, load_codes, limit_codes):
    injections = (load_codes.astype(jnp.float32) / 1024.0).astype(jnp.bfloat16)
    flows = jnp.dot(ptdf, injections, preferred_element_type=jnp.float32)
    limits = (limit_codes.astype(jnp.float32) / 64.0)[:, None]
    magnitude = jnp.sqrt(flows * flows + 1.0)
    zvalue = 4.0 * (magnitude / limits - 1.0)
    penalty = jax.nn.softplus(zvalue) / 4.0
    adjoint = (jax.nn.sigmoid(zvalue) * flows / (magnitude * limits)).astype(jnp.bfloat16)
    sensitivity = lax.dot_general(ptdf, adjoint, (((0,), (0,)), ((), ())), preferred_element_type=jnp.float32)
    return (penalty, sensitivity)
```

```python
import jax
import jax.numpy as jnp
from jax import lax
from jax.sharding import PartitionSpec as P


def overload(flows, limit_codes):
    limits = (limit_codes.astype(jnp.float32) / 64.0)[:, None]
    magnitude = jnp.sqrt(flows * flows + 1.0)
    zvalue = 4.0 * (magnitude / limits - 1.0)
    penalty = jax.nn.softplus(zvalue) / 4.0
    adjoint = (jax.nn.sigmoid(zvalue) * flows / (magnitude * limits)).astype(jnp.bfloat16)
    return (penalty, adjoint)


def local(ptdf, load_codes, limit_codes):
    injections = (load_codes.astype(jnp.float32) / 1024.0).astype(jnp.bfloat16)
    branch_local = ptdf.shape[0]
    owned = branch_local // lax.axis_size("bus")
    offset = lax.axis_index("bus") * owned
    partial_flows = jnp.dot(ptdf, injections, preferred_element_type=jnp.float32)
    flows = lax.psum_scatter(partial_flows, "bus", scatter_dimension=0, tiled=True)
    limits_own = lax.dynamic_slice_in_dim(limit_codes, offset, owned, 0)
    penalty, adjoint_own = overload(flows, limits_own)
    adjoint_block = lax.all_gather(adjoint_own, "bus", axis=0, tiled=True)
    partial_sens = lax.dot_general(
        ptdf, adjoint_block, (((0,), (0,)), ((), ())), preferred_element_type=jnp.float32
    )
    sensitivity = lax.psum_scatter(partial_sens, "br", scatter_dimension=1, tiled=True)
    return (penalty, sensitivity)


def solution(mesh):
    return jax.shard_map(
        local,
        mesh=mesh,
        in_specs=(P("br", "bus"), P("bus", None), P("br")),
        out_specs=(P(("br", "bus"), None), P("bus", "br")),
        check_vma=False,
    )
```

```python
import jax
import jax.numpy as jnp
from jax import lax
from jax.experimental import pallas as pl
from jax.experimental.pallas import tpu as pltpu
from jax.sharding import PartitionSpec as P

MESH = pl.DeviceIdType.MESH
NX, NYL, NYH, NZ, NC = 4, 2, 2, 8, 2
LANES = 128
F32, BF16 = jnp.float32, jnp.bfloat16


def epilogue(flows, limits):
    magnitude = jnp.sqrt(flows * flows + 1.0)
    zvalue = 4.0 * (magnitude / limits - 1.0)
    decay = jnp.exp(-jnp.abs(zvalue))
    penalty = (jnp.maximum(zvalue, 0.0) + jnp.log1p(decay)) * 0.25
    sigmoid = jnp.where(zvalue >= 0.0, 1.0, decay) / (1.0 + decay)
    adjoint = sigmoid * flows / (magnitude * limits)
    return penalty, adjoint


def kernel(
    ptdf, codes, limits, penalty_out, sens_out,
    p_v, pt_v, codes_v, inj_v, part, core_in, y_out, y_in, z_out, z_in, z_own, adj, pen_v,
    opp_out, opp_in, right_out, left_out, right_in, left_in, pair_own, pair_out, pair_in, sens_v,
    p_sem, c_sem, core_sem, y_sem, zs_sem, zr_sem, gzs_sem, gzr_sem, gy_sem, gc_sem,
    opp_sem, right_sem, left_sem, pair_sem, pen_sem, sens_sem,
):
    br, bus = lax.axis_index("br"), lax.axis_index("bus")
    x, ylo = lax.rem(br, NX), br // NX
    core, z, yhi = lax.rem(bus, NC), lax.rem(bus // NC, NZ), bus // (NC * NZ)
    rows = p_v.shape[0]
    buses = p_v.shape[1]
    own = rows // (NYH * NZ * NC)
    width = NYL * LANES
    steps = opp_out.shape[1]
    tile = opp_out.shape[2]
    half = steps * tile

    def at_bus(h, zz, c):
        return (br, (h * NZ + zz) * NC + c)

    sibling = at_bus(yhi, z, 1 - core)
    far_y = at_bus(1 - yhi, z, core)

    def z_peer(d):
        return at_bus(yhi, lax.rem(z + d, NZ), core)

    right = (ylo * NX + lax.rem(x + 1, NX), bus)
    left = (ylo * NX + lax.rem(x + NX - 1, NX), bus)
    pair = ((1 - ylo) * NX + x, bus)
    partners = [sibling, far_y, right, left, pair] + [z_peer(d) for d in range(1, NZ)]

    def block_of(k):
        return lax.rem(x + (2, 1, 3, 0)[k], NX)

    def columns(k, b):
        return pl.ds(pl.multiple_of((block_of(k) + b * NX) * LANES, LANES), LANES)

    def remote(src, dst, send, recv, device):
        return pltpu.make_async_remote_copy(
            src_ref=src, dst_ref=dst, send_sem=send, recv_sem=recv, device_id=device, device_id_type=MESH
        )

    ptile = rows // 4

    def p_copy(i):
        s = pl.ds(i * ptile, ptile)
        return pltpu.make_async_copy(ptdf.at[s], p_v.at[s], p_sem.at[i])

    def codes_copy(k, b):
        return pltpu.make_async_copy(codes.at[:, columns(k, b)], codes_v.at[k, b], c_sem.at[k, b])

    for b in range(NYL):
        codes_copy(0, b).start()
    for i in range(4):
        p_copy(i).start()

    barrier = pltpu.get_barrier_semaphore()
    for device in partners:
        pl.semaphore_signal(barrier, inc=1, device_id=device, device_id_type=MESH)
    pl.semaphore_wait(barrier, len(partners))

    def core_copy(k):
        return remote(part.at[k, :, :, 1 - core], core_in.at[k], core_sem.at[0, k], core_sem.at[1, k], sibling)

    def y_copy(k):
        return remote(y_out.at[k], y_in.at[k], y_sem.at[0, k], y_sem.at[1, k], far_y)

    def z_copy(k, d):
        return remote(
            z_out.at[k, lax.rem(z + d, NZ)], z_in.at[k, d - 1], zs_sem.at[k, d - 1], zr_sem.at[k, d - 1], z_peer(d)
        )

    def gz_copy(k, d):
        mine = adj.at[k, yhi, z, core]
        return remote(mine, mine, gzs_sem.at[k, d - 1], gzr_sem.at[k, d - 1], z_peer(d))

    def gz_arrival(k, d):
        theirs = adj.at[k, yhi, lax.rem(z + NZ - d, NZ), core]
        return remote(theirs, theirs, gzs_sem.at[k, d - 1], gzr_sem.at[k, d - 1], z_peer(d))

    def gy_copy(k, h):
        rows_of = adj.at[k, h, :, core]
        return remote(rows_of, rows_of, gy_sem.at[0, k], gy_sem.at[1, k], far_y)

    def gc_copy(k, near, c):
        rows_of = adj.at[k, yhi if near else 1 - yhi, :, c]
        which = 0 if near else 1
        return remote(rows_of, rows_of, gc_sem.at[0, k, which], gc_sem.at[1, k, which], sibling)

    def stage_matmul(k):
        for b in range(NYL):
            codes_copy(k, b).wait()
        if k + 1 < NX:
            for b in range(NYL):
                codes_copy(k + 1, b).start()
        strip = 256

        def convert(i, _):
            s = pl.ds(pl.multiple_of(i * strip, strip), strip)
            for b in range(NYL):
                values = codes_v[k, b, s].astype(F32) * (1.0 / 1024.0)
                inj_v[s, b * LANES : (b + 1) * LANES] = values.astype(BF16)
            return 0

        lax.fori_loop(0, buses // strip, convert, 0)
        group = ptile // (NC * own)
        for i in range(4):
            if k == 0:
                p_copy(i).wait()
            product = jnp.dot(p_v[i * ptile : (i + 1) * ptile], inj_v[...], preferred_element_type=F32)
            product = product.reshape(group, NC, own, width)
            first = i * group
            part[k, first // NZ, first % NZ : first % NZ + group] = product
        core_copy(k).start()

    def stage_core(k):
        core_copy(k).wait_recv()
        y_out[k] = (part[k, 1 - yhi, :, core] + core_in[k, 1 - yhi]).astype(BF16)
        y_copy(k).start()

    def stage_y(k):
        y_copy(k).wait_recv()
        total = part[k, yhi, :, core] + core_in[k, yhi] + y_in[k].astype(F32)
        part[k, yhi, :, core] = total
        z_out[k] = total.astype(BF16)
        for d in range(1, NZ):
            z_copy(k, d).start()
        z_own[k] = part[k, yhi, z, core]

    def stage_z(k):
        flows = z_own[k]
        for d in range(1, NZ):
            z_copy(k, d).wait_recv()
            flows = flows + z_in[k, d - 1].astype(F32)
        lim = limits[...]
        penalty, adjoint = epilogue(flows, jnp.concatenate([lim] * NYL, axis=1))
        adj[k, yhi, z, core] = adjoint.astype(BF16)
        for d in range(1, NZ):
            gz_copy(k, d).start()
        for b in range(NYL):
            pen_v[k, b] = penalty[:, b * LANES : (b + 1) * LANES]
            pen_copy(k, b).start()

    def pen_copy(k, b):
        return pltpu.make_async_copy(pen_v.at[k, b], penalty_out.at[:, columns(k, b)], pen_sem.at[k, b])

    def stage_gather_z(k):
        for d in range(1, NZ):
            gz_arrival(k, d).wait_recv()
        gy_copy(k, yhi).start()
        gc_copy(k, True, core).start()

    def stage_gather_y(k):
        gy_copy(k, 1 - yhi).wait_recv()
        gc_copy(k, False, core).start()

    def transpose_some(first, count):
        strip = 256

        def body(i, _):
            s = pl.ds(pl.multiple_of(i * strip, strip), strip)
            pt_v[s] = p_v[:, s].T
            return 0

        lax.fori_loop(first, first + count, body, 0)

    def product(k, row0):
        lhs = pt_v[pl.ds(pl.multiple_of(row0, tile), tile)]
        rhs = adj[k].reshape(rows, width)
        return jnp.dot(lhs, rhs, preferred_element_type=F32)

    def opp_copy(side, j):
        return remote(
            opp_out.at[side, j], opp_in.at[side, j], opp_sem.at[0, side, j], opp_sem.at[1, side, j], (right, left)[side]
        )

    def right_copy(i):
        return remote(right_out.at[i], right_in.at[i], right_sem.at[0, i], right_sem.at[1, i], right)

    def left_copy(i):
        return remote(left_out.at[i], left_in.at[i], left_sem.at[0, i], left_sem.at[1, i], left)

    def stage_block(k):
        gc_copy(k, True, 1 - core).wait_recv()
        gc_copy(k, False, 1 - core).wait_recv()

        def opposite(j, _):
            opp_out[0, j] = product(0, j * tile).astype(BF16)
            opp_copy(0, j).start()
            opp_out[1, j] = product(0, half + j * tile).astype(BF16)
            opp_copy(1, j).start()
            return 0

        def rightward(j, _):
            right_out[steps + j] = product(1, half + j * tile).astype(BF16)
            right_copy(steps + j).start()
            return 0

        def leftward(j, _):
            left_out[j] = product(2, j * tile).astype(BF16)
            left_copy(j).start()
            return 0

        if k < 3:
            lax.fori_loop(0, steps, (opposite, rightward, leftward)[k], 0)

    stages = [stage_matmul, stage_core, stage_y, stage_z, stage_gather_z, stage_gather_y, stage_block]
    strips = buses // 256
    for t in range(NX + len(stages) - 1):
        for s in reversed(range(len(stages))):
            if 0 <= t - s < NX:
                stages[s](t - s)
        if 1 <= t <= 4:
            transpose_some((t - 1) * strips // 4, strips // 4)

    def relay(j, _):
        mine = product(1, j * tile)
        opp_copy(0, j).wait_recv()
        right_out[j] = (mine + opp_in[0, j].astype(F32)).astype(BF16)
        right_copy(j).start()
        mine = product(2, half + j * tile)
        opp_copy(1, j).wait_recv()
        left_out[steps + j] = (mine + opp_in[1, j].astype(F32)).astype(BF16)
        left_copy(steps + j).start()
        return 0

    lax.fori_loop(0, steps, relay, 0)

    def pair_copy(i):
        return remote(pair_out.at[i], pair_in.at[i], pair_sem.at[0, i], pair_sem.at[1, i], pair)

    def sens_copy(i):
        return pltpu.make_async_copy(
            sens_v.at[i], sens_out.at[pl.ds(pl.multiple_of(i * tile, tile), tile)], sens_sem.at[i]
        )

    def reduce_x(i):
        total = product(3, i * tile)
        right_copy(i).wait_recv()
        left_copy(i).wait_recv()
        total = total + right_in[i].astype(F32) + left_in[i].astype(F32)
        first, second = total[:, :LANES], total[:, LANES:]
        low = ylo == 0
        pair_own[i] = jnp.where(low, first, second)
        pair_out[i] = jnp.where(low, second, first).astype(BF16)
        pair_copy(i).start()

    def finish(i):
        pair_copy(i).wait_recv()
        sens_v[i] = pair_own[i] + pair_in[i].astype(F32)
        sens_copy(i).start()

    def last(j, _):
        @pl.when(j < steps)
        def _():
            reduce_x(j)
            reduce_x(steps + j)

        @pl.when(j > 0)
        def _():
            finish(j - 1)
            finish(steps + j - 1)

        return 0

    lax.fori_loop(0, steps + 1, last, 0)

    for k in range(NX):
        core_copy(k).wait_send()
        y_copy(k).wait_send()
        gy_copy(k, yhi).wait_send()
        gc_copy(k, True, core).wait_send()
        gc_copy(k, False, core).wait_send()
        for d in range(1, NZ):
            z_copy(k, d).wait_send()
            gz_copy(k, d).wait_send()
        for b in range(NYL):
            pen_copy(k, b).wait()

    def drain(j, _):
        for side in range(2):
            opp_copy(side, j).wait_send()
            i = side * steps + j
            right_copy(i).wait_send()
            left_copy(i).wait_send()
            pair_copy(i).wait_send()
            sens_copy(i).wait()
        return 0

    lax.fori_loop(0, steps, drain, 0)


def local(ptdf, load_codes, limit_codes):
    rows, buses = ptdf.shape
    hours = load_codes.shape[1]
    own = rows // (NYH * NZ * NC)
    width = NYL * LANES
    tile = 128
    steps = buses // 2 // tile
    offset = lax.axis_index("bus") * own
    limits = lax.dynamic_slice_in_dim(limit_codes, offset, own, 0).astype(F32) / 64.0
    limits = jnp.broadcast_to(limits[:, None], (own, LANES))
    dma = pltpu.SemaphoreType.DMA
    scratch = [
        pltpu.VMEM((rows, buses), BF16),
        pltpu.VMEM((buses, rows), BF16),
        pltpu.VMEM((NX, NYL, buses, LANES), jnp.int32),
        pltpu.VMEM((buses, width), BF16),
        pltpu.VMEM((NX, NYH, NZ, NC, own, width), F32),
        pltpu.VMEM((NX, NYH, NZ, own, width), F32),
        pltpu.VMEM((NX, NZ, own, width), BF16),
        pltpu.VMEM((NX, NZ, own, width), BF16),
        pltpu.VMEM((NX, NZ, own, width), BF16),
        pltpu.VMEM((NX, NZ - 1, own, width), BF16),
        pltpu.VMEM((NX, own, width), F32),
        pltpu.VMEM((NX, NYH, NZ, NC, own, width), BF16),
        pltpu.VMEM((NX, NYL, own, LANES), F32),
        pltpu.VMEM((2, steps, tile, width), BF16),
        pltpu.VMEM((2, steps, tile, width), BF16),
        pltpu.VMEM((2 * steps, tile, width), BF16),
        pltpu.VMEM((2 * steps, tile, width), BF16),
        pltpu.VMEM((2 * steps, tile, width), BF16),
        pltpu.VMEM((2 * steps, tile, width), BF16),
        pltpu.VMEM((2 * steps, tile, LANES), F32),
        pltpu.VMEM((2 * steps, tile, LANES), BF16),
        pltpu.VMEM((2 * steps, tile, LANES), BF16),
        pltpu.VMEM((2 * steps, tile, LANES), F32),
        dma((4,)),
        dma((NX, NYL)),
        dma((2, NX)),
        dma((2, NX)),
        dma((NX, NZ - 1)),
        dma((NX, NZ - 1)),
        dma((NX, NZ - 1)),
        dma((NX, NZ - 1)),
        dma((2, NX)),
        dma((2, NX, 2)),
        dma((2, 2, steps)),
        dma((2, 2 * steps)),
        dma((2, 2 * steps)),
        dma((2, 2 * steps)),
        dma((NX, NYL)),
        dma((2 * steps,)),
    ]
    anywhere = pl.BlockSpec(memory_space=pl.ANY)
    return pl.pallas_call(
        kernel,
        out_shape=(
            jax.ShapeDtypeStruct((own, hours), F32),
            jax.ShapeDtypeStruct((buses, LANES), F32),
        ),
        in_specs=[anywhere, anywhere, pl.BlockSpec(memory_space=pltpu.VMEM)],
        out_specs=(anywhere, anywhere),
        scratch_shapes=scratch,
        compiler_params=pltpu.CompilerParams(
            collective_id=0, has_side_effects=True, vmem_limit_bytes=48 * 1024 * 1024
        ),
    )(ptdf, load_codes, limits)


def solution(mesh):
    return jax.shard_map(
        local,
        mesh=mesh,
        in_specs=(P("br", "bus"), P("bus", None), P("br")),
        out_specs=(P(("br", "bus"), None), P("bus", "br")),
        check_vma=False,
    )
```

```python
import jax
import jax.numpy as jnp
from jax import lax
from jax.experimental import pallas as pl
from jax.experimental.pallas import tpu as pltpu
from jax.sharding import PartitionSpec as P

MESH = pl.DeviceIdType.MESH
NX, NYL, NYH, NZ, NC = 4, 2, 2, 8, 2
LANES = 128
UNITS = 8
ORDER = (0, 1, 2, 4, 6, 3, 5, 7)
LAGS = (1, 3, 5, 7, 9, 10)
MATMULS = (0, 1, 2, 4)
RELAY_DELAY = (0, 0)
PAIR_DELAY = 2
F32, BF16 = jnp.float32, jnp.bfloat16


def epilogue(flows, limits):
    magnitude = jnp.sqrt(flows * flows + 1.0)
    zvalue = 4.0 * (magnitude / limits - 1.0)
    decay = jnp.exp(-jnp.abs(zvalue))
    penalty = (jnp.maximum(zvalue, 0.0) + jnp.log1p(decay)) * 0.25
    sigmoid = jnp.where(zvalue >= 0.0, 1.0, decay) / (1.0 + decay)
    adjoint = sigmoid * flows / (magnitude * limits)
    return penalty, adjoint


def kernel(
    ptdf, codes, limit_codes, penalty_out, sens_out,
    p_v, codes_v, inj_v, limit_s, limits, part, core_in, y_out, y_in, z_out, z_in, z_own, adj, pen_v, s_v,
    opp_out, opp_in, right_out, left_out, right_in, left_in, pair_out, pair_in, sens_v,
    p_sem, c_sem, l_sem, core_sem, y_sem, zs_sem, zr_sem, gzs_sem, gzr_sem, gy_sem, gc_sem,
    opp_sem, right_sem, left_sem, pair_sem, pen_sem, sens_sem,
):
    br, bus = lax.axis_index("br"), lax.axis_index("bus")
    x, ylo = lax.rem(br, NX), br // NX
    core, z, yhi = lax.rem(bus, NC), lax.rem(bus // NC, NZ), bus // (NC * NZ)
    rows, buses = p_v.shape
    own = rows // (NYH * NZ * NC)
    steps, tile = opp_out.shape[2], opp_out.shape[3]
    half = steps * tile

    def at_bus(h, zz, c):
        return (br, (h * NZ + zz) * NC + c)

    sibling = at_bus(yhi, z, 1 - core)
    far_y = at_bus(1 - yhi, z, core)

    def z_peer(d):
        return at_bus(yhi, lax.rem(z + d, NZ), core)

    right = (ylo * NX + lax.rem(x + 1, NX), bus)
    left = (ylo * NX + lax.rem(x + NX - 1, NX), bus)
    pair = ((1 - ylo) * NX + x, bus)
    partners = [sibling, far_y, right, left, pair] + [z_peer(d) for d in range(1, NZ)]

    def columns(u):
        k, s = u // 2, lax.rem(u, 2)
        ahead = jnp.where(k == 0, 2, jnp.where(k == 1, 1, jnp.where(k == 2, 3, 0)))
        block = lax.rem(x + ahead, NX) + NX * jnp.where(s == 0, 1 - ylo, ylo)
        return pl.ds(pl.multiple_of(block * LANES, LANES), LANES)

    def pick(index, choices):
        value = jnp.int32(choices[-1])
        for i, choice in enumerate(choices[:-1]):
            value = jnp.where(index == i, choice, value)
        return value

    def remote(src, dst, send, recv, device):
        return pltpu.make_async_remote_copy(
            src_ref=src, dst_ref=dst, send_sem=send, recv_sem=recv, device_id=device, device_id_type=MESH
        )

    def codes_copy(u):
        return pltpu.make_async_copy(codes.at[:, columns(u)], codes_v.at[u], c_sem.at[u])

    p_copy = pltpu.make_async_copy(ptdf, p_v, p_sem)
    limit_copy = pltpu.make_async_copy(limit_codes, limit_s, l_sem)
    codes_copy(jnp.int32(0)).start()
    codes_copy(jnp.int32(1)).start()
    p_copy.start()
    limit_copy.start()
    barrier = pltpu.get_barrier_semaphore()
    for device in partners:
        pl.semaphore_signal(barrier, inc=1, device_id=device, device_id_type=MESH)
    pl.semaphore_wait(barrier, len(partners))

    def core_copy(u):
        return remote(part.at[u, :, :, 1 - core], core_in.at[u], core_sem.at[0, u], core_sem.at[1, u], sibling)

    def y_copy(u):
        return remote(y_out.at[u], y_in.at[u], y_sem.at[0, u], y_sem.at[1, u], far_y)

    def z_copy(u, d):
        return remote(
            z_out.at[u, lax.rem(z + d, NZ)], z_in.at[u, d - 1], zs_sem.at[u, d - 1], zr_sem.at[u, d - 1], z_peer(d)
        )

    def gz_copy(u, d):
        mine = adj.at[u, yhi, z, core]
        return remote(mine, mine, gzs_sem.at[u, d - 1], gzr_sem.at[u, d - 1], z_peer(d))

    def gz_arrival(u, d):
        theirs = adj.at[u, yhi, lax.rem(z + NZ - d, NZ), core]
        return remote(theirs, theirs, gzs_sem.at[u, d - 1], gzr_sem.at[u, d - 1], z_peer(d))

    def gy_copy(u, h):
        rows_of = adj.at[u, h, :, core]
        return remote(rows_of, rows_of, gy_sem.at[0, u], gy_sem.at[1, u], far_y)

    def gc_copy(u, near, c):
        rows_of = adj.at[u, yhi if near else 1 - yhi, :, c]
        which = 0 if near else 1
        return remote(rows_of, rows_of, gc_sem.at[0, u, which], gc_sem.at[1, u, which], sibling)

    def pen_copy(u):
        return pltpu.make_async_copy(pen_v.at[u], penalty_out.at[:, columns(u)], pen_sem.at[u])

    def stage_matmul(k):
        strip = 256
        for s in range(2):
            codes_copy(2 * k + s).wait()

        def convert(i, _):
            at = pl.ds(pl.multiple_of(i * strip, strip), strip)
            for s in range(2):
                values = codes_v[2 * k + s, at].astype(F32) * (1.0 / 1024.0)
                inj_v[at, s * LANES : (s + 1) * LANES] = values.astype(BF16)
            return 0

        lax.fori_loop(0, buses // strip, convert, 0)
        @pl.when(k == 0)
        def _():
            p_copy.wait()
            for u in range(2, UNITS):
                codes_copy(jnp.int32(u)).start()

        product = jnp.dot(p_v[...], inj_v[...], preferred_element_type=F32)
        for s in range(2):
            part[2 * k + s] = product[:, s * LANES : (s + 1) * LANES].reshape(NYH, NZ, NC, own, LANES)

        for s in range(2):
            core_copy(2 * k + s).start()

        @pl.when(k == 0)
        def _():
            limit_copy.wait()
            row = lax.broadcasted_iota(jnp.int32, (own, LANES), 0)
            values = jnp.zeros((own, LANES), F32)
            for i in range(own):
                values = jnp.where(row == i, limit_s[bus * own + i].astype(F32), values)
            limits[...] = values * (1.0 / 64.0)

    def stage_core(u):
        core_copy(u).wait_recv()
        y_out[u] = (part[u, 1 - yhi, :, core] + core_in[u, 1 - yhi]).astype(BF16)
        y_copy(u).start()

    def stage_y(u):
        y_copy(u).wait_recv()
        total = part[u, yhi, :, core] + core_in[u, yhi] + y_in[u].astype(F32)
        part[u, yhi, :, core] = total
        z_out[u] = total.astype(BF16)
        for d in range(1, NZ):
            z_copy(u, d).start()
        z_own[u] = part[u, yhi, z, core]

    def stage_z(u):
        flows = z_own[u]
        for d in range(1, NZ):
            z_copy(u, d).wait_recv()
            flows = flows + z_in[u, d - 1].astype(F32)
        penalty, adjoint = epilogue(flows, limits[...])
        adj[u, yhi, z, core] = adjoint.astype(BF16)
        for d in range(1, NZ):
            gz_copy(u, d).start()
        pen_v[u] = penalty
        pen_copy(u).start()

    def stage_gather_z(u):
        for d in range(1, NZ):
            gz_arrival(u, d).wait_recv()
        gy_copy(u, yhi).start()
        gc_copy(u, True, core).start()

    def stage_gather_y(u):
        gy_copy(u, 1 - yhi).wait_recv()
        gc_copy(u, False, core).start()

    def opp_copy(s, side, j):
        return remote(
            opp_out.at[s, side, j], opp_in.at[s, side, j], opp_sem.at[0, s, side, j], opp_sem.at[1, s, side, j],
            (right, left)[side],
        )

    def right_copy(s, i):
        return remote(right_out.at[s, i], right_in.at[s, i], right_sem.at[0, s, i], right_sem.at[1, s, i], right)

    def left_copy(s, i):
        return remote(left_out.at[s, i], left_in.at[s, i], left_sem.at[0, s, i], left_sem.at[1, s, i], left)

    def tile_at(i):
        return pl.ds(pl.multiple_of(i * tile, tile), tile)

    def stage_sens(u):
        gc_copy(u, True, 1 - core).wait_recv()
        gc_copy(u, False, 1 - core).wait_recv()
        k, s = u // 2, lax.rem(u, 2)
        rhs = adj[u].reshape(rows, LANES)
        s_v[u] = lax.dot_general(p_v[...], rhs, (((0,), (0,)), ((), ())), preferred_element_type=F32)

        def opposite(j, _):
            opp_out[s, 0, j] = s_v[u, tile_at(j)].astype(BF16)
            opp_copy(s, 0, j).start()
            opp_out[s, 1, j] = s_v[u, tile_at(steps + j)].astype(BF16)
            opp_copy(s, 1, j).start()
            return 0

        def rightward(j, _):
            right_out[s, steps + j] = s_v[u, tile_at(steps + j)].astype(BF16)
            right_copy(s, steps + j).start()
            return 0

        def leftward(j, _):
            left_out[s, j] = s_v[u, tile_at(j)].astype(BF16)
            left_copy(s, j).start()
            return 0

        for kind, send in enumerate((opposite, rightward, leftward)):

            @pl.when(k == kind)
            def _(send=send):
                lax.fori_loop(0, steps, send, 0)

    def relay(s):
        def body(j, _):
            opp_copy(s, 0, j).wait_recv()
            right_out[s, j] = (s_v[2 + s, tile_at(j)] + opp_in[s, 0, j].astype(F32)).astype(BF16)
            right_copy(s, j).start()
            opp_copy(s, 1, j).wait_recv()
            left_out[s, steps + j] = (s_v[4 + s, tile_at(steps + j)] + opp_in[s, 1, j].astype(F32)).astype(BF16)
            left_copy(s, steps + j).start()
            return 0

        lax.fori_loop(0, steps, body, 0)

    stages = [stage_core, stage_y, stage_z, stage_gather_z, stage_gather_y, stage_sens]
    def pair_copy(i):
        return remote(pair_out.at[i], pair_in.at[i], pair_sem.at[0, i], pair_sem.at[1, i], pair)

    def sens_copy(i):
        return pltpu.make_async_copy(sens_v.at[i], sens_out.at[tile_at(i)], sens_sem.at[i])

    def x_sum(s, i):
        right_copy(s, i).wait_recv()
        left_copy(s, i).wait_recv()
        return s_v[6 + s, tile_at(i)] + right_in[s, i].astype(F32) + left_in[s, i].astype(F32)

    def for_pair(j, _):
        for i in (j, steps + j):
            pair_out[i] = x_sum(0, i).astype(BF16)
            pair_copy(i).start()
        return 0

    def for_self(j, _):
        for i in (j, steps + j):
            total = x_sum(1, i)
            pair_copy(i).wait_recv()
            sens_v[i] = total + pair_in[i].astype(F32)
            sens_copy(i).start()
        return 0

    waits = {unit: ORDER.index(unit) + LAGS[-1] for unit in range(UNITS)}
    relay_at = [max(waits[2 + s], waits[4 + s]) + RELAY_DELAY[s] for s in range(2)]
    pair_at = max(relay_at[0], waits[6]) + PAIR_DELAY

    def run(t, _):
        for lag, stage in reversed(list(zip(LAGS, stages))):
            p = t - lag

            @pl.when((p >= 0) & (p < UNITS))
            def _(p=p, stage=stage):
                stage(pick(p, ORDER))

        this = sum(jnp.where(t == at, k, 0) for k, at in enumerate(MATMULS))

        @pl.when((this > 0) | (t == MATMULS[0]))
        def _():
            stage_matmul(this)

        @pl.when((t == relay_at[0]) | (t == relay_at[1]))
        def _():
            relay(jnp.where(t == relay_at[0], 0, 1))

        @pl.when(t == pair_at)
        def _():
            lax.fori_loop(0, steps, for_pair, 0)

        return 0

    lax.fori_loop(0, max(UNITS + LAGS[-1], relay_at[1] + 1, pair_at + 1), run, 0)
    lax.fori_loop(0, steps, for_self, 0)

    def drain_unit(u, _):
        core_copy(u).wait_send()
        y_copy(u).wait_send()
        gy_copy(u, yhi).wait_send()
        gc_copy(u, True, core).wait_send()
        gc_copy(u, False, core).wait_send()
        for d in range(1, NZ):
            z_copy(u, d).wait_send()
            gz_copy(u, d).wait_send()
        pen_copy(u).wait()
        return 0

    lax.fori_loop(0, UNITS, drain_unit, 0)

    def drain(j, _):
        for side in range(2):
            i = side * steps + j
            for s in range(2):
                opp_copy(s, side, j).wait_send()
                right_copy(s, i).wait_send()
                left_copy(s, i).wait_send()
            pair_copy(i).wait_send()
            sens_copy(i).wait()
        return 0

    lax.fori_loop(0, steps, drain, 0)


def local(ptdf, load_codes, limit_codes):
    rows, buses = ptdf.shape
    hours = load_codes.shape[1]
    own = rows // (NYH * NZ * NC)
    tile = 256
    steps = buses // 2 // tile
    dma = pltpu.SemaphoreType.DMA
    piece = (UNITS, NZ, own, LANES)
    tiles = (2, 2 * steps, tile, LANES)
    scratch = [
        pltpu.VMEM((rows, buses), BF16),
        pltpu.VMEM((UNITS, buses, LANES), jnp.int32),
        pltpu.VMEM((buses, 2 * LANES), BF16),
        pltpu.SMEM((rows,), jnp.int32),
        pltpu.VMEM((own, LANES), F32),
        pltpu.VMEM((UNITS, NYH, NZ, NC, own, LANES), F32),
        pltpu.VMEM((UNITS, NYH, NZ, own, LANES), F32),
        pltpu.VMEM(piece, BF16),
        pltpu.VMEM(piece, BF16),
        pltpu.VMEM(piece, BF16),
        pltpu.VMEM((UNITS, NZ - 1, own, LANES), BF16),
        pltpu.VMEM((UNITS, own, LANES), F32),
        pltpu.VMEM((UNITS, NYH, NZ, NC, own, LANES), BF16),
        pltpu.VMEM((UNITS, own, LANES), F32),
        pltpu.VMEM((UNITS, buses, LANES), F32),
        pltpu.VMEM((2, 2, steps, tile, LANES), BF16),
        pltpu.VMEM((2, 2, steps, tile, LANES), BF16),
        pltpu.VMEM(tiles, BF16),
        pltpu.VMEM(tiles, BF16),
        pltpu.VMEM(tiles, BF16),
        pltpu.VMEM(tiles, BF16),
        pltpu.VMEM(tiles[1:], BF16),
        pltpu.VMEM(tiles[1:], BF16),
        pltpu.VMEM(tiles[1:], F32),
        dma,
        dma((UNITS,)),
        dma,
        dma((2, UNITS)),
        dma((2, UNITS)),
        dma((UNITS, NZ - 1)),
        dma((UNITS, NZ - 1)),
        dma((UNITS, NZ - 1)),
        dma((UNITS, NZ - 1)),
        dma((2, UNITS)),
        dma((2, UNITS, 2)),
        dma((2, 2, 2, steps)),
        dma((2, 2, 2 * steps)),
        dma((2, 2, 2 * steps)),
        dma((2, 2 * steps)),
        dma((UNITS,)),
        dma((2 * steps,)),
    ]
    anywhere = pl.BlockSpec(memory_space=pl.ANY)
    return pl.pallas_call(
        kernel,
        out_shape=(
            jax.ShapeDtypeStruct((own, hours), F32),
            jax.ShapeDtypeStruct((buses, LANES), F32),
        ),
        in_specs=[anywhere] * 3,
        out_specs=(anywhere, anywhere),
        scratch_shapes=scratch,
        compiler_params=pltpu.CompilerParams(
            collective_id=0, has_side_effects=True, vmem_limit_bytes=42 * 1024 * 1024
        ),
    )(ptdf, load_codes, limit_codes)


def solution(mesh):
    return jax.shard_map(
        local,
        mesh=mesh,
        in_specs=(P("br", "bus"), P("bus", None), P("br")),
        out_specs=(P(("br", "bus"), None), P("bus", "br")),
        check_vma=False,
    )
```

```python
import jax
import jax.numpy as jnp
from jax import lax
from jax.experimental import pallas as pl
from jax.experimental.pallas import tpu as pltpu
from jax.sharding import PartitionSpec as P

MESH = pl.DeviceIdType.MESH
NX, NYL, NYH, NZ, NC = 4, 2, 2, 8, 2
LANES = 128
UNITS = 8
ORDER = (0, 1, 2, 4, 6, 3, 5, 7)
LAGS = (1, 3, 5, 7, 9, 10)
MATMULS = (0, 1, 2, 4)
RELAY_DELAY = (0, 0)
PAIR_DELAY = 2
F32, BF16 = jnp.float32, jnp.bfloat16


def epilogue(flows, limits):
    magnitude = jnp.sqrt(flows * flows + 1.0)
    zvalue = 4.0 * (magnitude / limits - 1.0)
    decay = jnp.exp(-jnp.abs(zvalue))
    penalty = (jnp.maximum(zvalue, 0.0) + jnp.log1p(decay)) * 0.25
    sigmoid = jnp.where(zvalue >= 0.0, 1.0, decay) / (1.0 + decay)
    adjoint = sigmoid * flows / (magnitude * limits)
    return penalty, adjoint


def kernel(
    ptdf, codes, limit_codes, penalty_out, sens_out,
    p_v, codes_v, inj_v, limit_s, limits, part, core_in, y_out, y_in, z_out, z_in, z_own, adj, pen_v, s_v,
    opp_out, opp_in, right_out, left_out, right_in, left_in, pair_out, pair_in, sens_v,
    p_sem, c_sem, l_sem, core_sem, y_sem, zs_sem, zr_sem, gzs_sem, gzr_sem, gy_sem, gc_sem,
    opp_sem, right_sem, left_sem, pair_sem, pen_sem, sens_sem,
):
    br, bus = lax.axis_index("br"), lax.axis_index("bus")
    x, ylo = lax.rem(br, NX), br // NX
    core, z, yhi = lax.rem(bus, NC), lax.rem(bus // NC, NZ), bus // (NC * NZ)
    rows, buses = p_v.shape
    own = rows // (NYH * NZ * NC)
    steps, tile = opp_out.shape[2], opp_out.shape[3]
    half = steps * tile

    def at_bus(h, zz, c):
        return (br, (h * NZ + zz) * NC + c)

    sibling = at_bus(yhi, z, 1 - core)
    far_y = at_bus(1 - yhi, z, core)

    z_peers = [at_bus(yhi, lax.rem(z + d, NZ), core) for d in range(NZ)]
    right = (ylo * NX + lax.rem(x + 1, NX), bus)
    left = (ylo * NX + lax.rem(x + NX - 1, NX), bus)
    pair = ((1 - ylo) * NX + x, bus)
    partners = [sibling, far_y, right, left, pair] + z_peers[1:]

    def columns(u):
        k, s = u // 2, lax.rem(u, 2)
        ahead = jnp.where(k == 0, 2, jnp.where(k == 1, 1, jnp.where(k == 2, 3, 0)))
        block = lax.rem(x + ahead, NX) + NX * jnp.where(s == 0, 1 - ylo, ylo)
        return pl.ds(pl.multiple_of(block * LANES, LANES), LANES)

    def pick(index, choices):
        value = jnp.int32(choices[-1])
        for i, choice in enumerate(choices[:-1]):
            value = jnp.where(index == i, choice, value)
        return value

    def remote(src, dst, send, recv, device):
        return pltpu.make_async_remote_copy(
            src_ref=src, dst_ref=dst, send_sem=send, recv_sem=recv, device_id=device, device_id_type=MESH
        )

    def codes_copy(u):
        return pltpu.make_async_copy(codes.at[:, columns(u)], codes_v.at[u], c_sem.at[u])

    p_copy = pltpu.make_async_copy(ptdf, p_v, p_sem)
    limit_copy = pltpu.make_async_copy(limit_codes, limit_s, l_sem)
    codes_copy(jnp.int32(0)).start()
    codes_copy(jnp.int32(1)).start()
    p_copy.start()
    limit_copy.start()
    barrier = pltpu.get_barrier_semaphore()
    for device in partners:
        pl.semaphore_signal(barrier, inc=1, device_id=device, device_id_type=MESH)
    pl.semaphore_wait(barrier, len(partners))

    def core_copy(u):
        return remote(part.at[u, :, :, 1 - core], core_in.at[u], core_sem.at[0, u], core_sem.at[1, u], sibling)

    def y_copy(u):
        return remote(y_out.at[u], y_in.at[u], y_sem.at[0, u], y_sem.at[1, u], far_y)

    def z_copy(u, d):
        return remote(
            z_out.at[u, lax.rem(z + d, NZ)], z_in.at[u, d - 1], zs_sem.at[u], zr_sem.at[u], z_peers[d]
        )

    def gz_copy(u, d):
        mine = adj.at[u, yhi, z, core]
        return remote(mine, mine, gzs_sem.at[u], gzr_sem.at[u], z_peers[d])

    def all_z(u, send, recv):
        return remote(z_in.at[u], z_in.at[u], send.at[u], recv.at[u], z_peers[1])

    def gy_copy(u, h):
        rows_of = adj.at[u, h, :, core]
        return remote(rows_of, rows_of, gy_sem.at[0, u], gy_sem.at[1, u], far_y)

    def gc_copy(u, near, c):
        rows_of = adj.at[u, yhi if near else 1 - yhi, :, c]
        which = 0 if near else 1
        return remote(rows_of, rows_of, gc_sem.at[0, u, which], gc_sem.at[1, u, which], sibling)

    def pen_copy(u):
        return pltpu.make_async_copy(pen_v.at[u], penalty_out.at[:, columns(u)], pen_sem.at[u])

    def stage_matmul(k):
        strip = 256
        for s in range(2):
            codes_copy(2 * k + s).wait()

        def convert(i, _):
            at = pl.ds(pl.multiple_of(i * strip, strip), strip)
            for s in range(2):
                values = codes_v[2 * k + s, at].astype(F32) * (1.0 / 1024.0)
                inj_v[at, s * LANES : (s + 1) * LANES] = values.astype(BF16)
            return 0

        lax.fori_loop(0, buses // strip, convert, 0)
        @pl.when(k == 0)
        def _():
            p_copy.wait()
            for u in range(2, UNITS):
                codes_copy(jnp.int32(u)).start()

        product = jnp.dot(p_v[...], inj_v[...], preferred_element_type=F32)
        for s in range(2):
            part[2 * k + s] = product[:, s * LANES : (s + 1) * LANES].reshape(NYH, NZ, NC, own, LANES)

        for s in range(2):
            core_copy(2 * k + s).start()

        @pl.when(k == 0)
        def _():
            limit_copy.wait()
            row = lax.broadcasted_iota(jnp.int32, (own, LANES), 0)
            values = jnp.zeros((own, LANES), F32)
            for i in range(own):
                values = jnp.where(row == i, limit_s[bus * own + i].astype(F32), values)
            limits[...] = values * (1.0 / 64.0)

    def stage_core(u):
        core_copy(u).wait_recv()
        y_out[u] = (part[u, 1 - yhi, :, core] + core_in[u, 1 - yhi]).astype(BF16)
        y_copy(u).start()

    def stage_y(u):
        y_copy(u).wait_recv()
        total = part[u, yhi, :, core] + core_in[u, yhi] + y_in[u].astype(F32)
        part[u, yhi, :, core] = total
        z_out[u] = total.astype(BF16)
        for d in (4, 3, 5, 2, 6, 1, 7):
            z_copy(u, d).start()
        z_own[u] = part[u, yhi, z, core]

    def stage_z(u):
        flows = z_own[u]
        all_z(u, zs_sem, zr_sem).wait_recv()
        for d in range(1, NZ):
            flows = flows + z_in[u, d - 1].astype(F32)
        penalty, adjoint = epilogue(flows, limits[...])
        adj[u, yhi, z, core] = adjoint.astype(BF16)
        for d in (4, 3, 5, 2, 6, 1, 7):
            gz_copy(u, d).start()
        pen_v[u] = penalty
        pen_copy(u).start()

    def stage_gather_z(u):
        all_z(u, gzs_sem, gzr_sem).wait_recv()
        gy_copy(u, yhi).start()
        gc_copy(u, True, core).start()

    def stage_gather_y(u):
        gy_copy(u, 1 - yhi).wait_recv()
        gc_copy(u, False, core).start()

    def opp_copy(s, side, j):
        return remote(
            opp_out.at[s, side, j], opp_in.at[s, side, j], opp_sem.at[0, s, side, j], opp_sem.at[1, s, side, j],
            (right, left)[side],
        )

    def right_copy(s, i):
        return remote(right_out.at[s, i], right_in.at[s, i], right_sem.at[0, s, i], right_sem.at[1, s, i], right)

    def left_copy(s, i):
        return remote(left_out.at[s, i], left_in.at[s, i], left_sem.at[0, s, i], left_sem.at[1, s, i], left)

    def tile_at(i):
        return pl.ds(pl.multiple_of(i * tile, tile), tile)

    def stage_sens(u):
        gc_copy(u, True, 1 - core).wait_recv()
        gc_copy(u, False, 1 - core).wait_recv()
        k, s = u // 2, lax.rem(u, 2)
        rhs = adj[u].reshape(rows, LANES)
        s_v[u] = lax.dot_general(p_v[...], rhs, (((0,), (0,)), ((), ())), preferred_element_type=F32)

        def opposite(j, _):
            opp_out[s, 0, j] = s_v[u, tile_at(j)].astype(BF16)
            opp_copy(s, 0, j).start()
            opp_out[s, 1, j] = s_v[u, tile_at(steps + j)].astype(BF16)
            opp_copy(s, 1, j).start()
            return 0

        def rightward(j, _):
            right_out[s, steps + j] = s_v[u, tile_at(steps + j)].astype(BF16)
            right_copy(s, steps + j).start()
            return 0

        def leftward(j, _):
            left_out[s, j] = s_v[u, tile_at(j)].astype(BF16)
            left_copy(s, j).start()
            return 0

        for kind, send in enumerate((opposite, rightward, leftward)):

            @pl.when(k == kind)
            def _(send=send):
                lax.fori_loop(0, steps, send, 0)

    def relay(s):
        def body(j, _):
            opp_copy(s, 0, j).wait_recv()
            right_out[s, j] = (s_v[2 + s, tile_at(j)] + opp_in[s, 0, j].astype(F32)).astype(BF16)
            right_copy(s, j).start()
            opp_copy(s, 1, j).wait_recv()
            left_out[s, steps + j] = (s_v[4 + s, tile_at(steps + j)] + opp_in[s, 1, j].astype(F32)).astype(BF16)
            left_copy(s, steps + j).start()
            return 0

        lax.fori_loop(0, steps, body, 0)

    stages = [stage_core, stage_y, stage_z, stage_gather_z, stage_gather_y, stage_sens]
    def pair_copy(i):
        return remote(pair_out.at[i], pair_in.at[i], pair_sem.at[0, i], pair_sem.at[1, i], pair)

    def sens_copy(i):
        return pltpu.make_async_copy(sens_v.at[i], sens_out.at[tile_at(i)], sens_sem.at[i])

    def x_sum(s, i):
        right_copy(s, i).wait_recv()
        left_copy(s, i).wait_recv()
        return s_v[6 + s, tile_at(i)] + right_in[s, i].astype(F32) + left_in[s, i].astype(F32)

    def for_pair(j, _):
        for i in (j, steps + j):
            pair_out[i] = x_sum(0, i).astype(BF16)
            pair_copy(i).start()
        return 0

    def for_self(j, _):
        for i in (j, steps + j):
            total = x_sum(1, i)
            pair_copy(i).wait_recv()
            sens_v[i] = total + pair_in[i].astype(F32)
            sens_copy(i).start()
        return 0

    waits = {unit: ORDER.index(unit) + LAGS[-1] for unit in range(UNITS)}
    relay_at = [max(waits[2 + s], waits[4 + s]) + RELAY_DELAY[s] for s in range(2)]
    pair_at = max(relay_at[0], waits[6]) + PAIR_DELAY

    def run(t, _):
        for lag, stage in reversed(list(zip(LAGS, stages))):
            p = t - lag

            @pl.when((p >= 0) & (p < UNITS))
            def _(p=p, stage=stage):
                stage(pick(p, ORDER))

        this = sum(jnp.where(t == at, k, 0) for k, at in enumerate(MATMULS))

        @pl.when((this > 0) | (t == MATMULS[0]))
        def _():
            stage_matmul(this)

        @pl.when((t == relay_at[0]) | (t == relay_at[1]))
        def _():
            relay(jnp.where(t == relay_at[0], 0, 1))

        @pl.when(t == pair_at)
        def _():
            lax.fori_loop(0, steps, for_pair, 0)

        return 0

    lax.fori_loop(0, max(UNITS + LAGS[-1], relay_at[1] + 1, pair_at + 1), run, 0)
    lax.fori_loop(0, steps, for_self, 0)

    def drain_unit(u, _):
        core_copy(u).wait_send()
        y_copy(u).wait_send()
        gy_copy(u, yhi).wait_send()
        gc_copy(u, True, core).wait_send()
        gc_copy(u, False, core).wait_send()
        all_z(u, zs_sem, zr_sem).wait_send()
        all_z(u, gzs_sem, gzr_sem).wait_send()
        pen_copy(u).wait()
        return 0

    lax.fori_loop(0, UNITS, drain_unit, 0)

    def drain(j, _):
        for side in range(2):
            i = side * steps + j
            for s in range(2):
                opp_copy(s, side, j).wait_send()
                right_copy(s, i).wait_send()
                left_copy(s, i).wait_send()
            pair_copy(i).wait_send()
            sens_copy(i).wait()
        return 0

    lax.fori_loop(0, steps, drain, 0)


def local(ptdf, load_codes, limit_codes):
    rows, buses = ptdf.shape
    hours = load_codes.shape[1]
    own = rows // (NYH * NZ * NC)
    tile = 512
    steps = buses // 2 // tile
    dma = pltpu.SemaphoreType.DMA
    piece = (UNITS, NZ, own, LANES)
    tiles = (2, 2 * steps, tile, LANES)
    scratch = [
        pltpu.VMEM((rows, buses), BF16),
        pltpu.VMEM((UNITS, buses, LANES), jnp.int32),
        pltpu.VMEM((buses, 2 * LANES), BF16),
        pltpu.SMEM((rows,), jnp.int32),
        pltpu.VMEM((own, LANES), F32),
        pltpu.VMEM((UNITS, NYH, NZ, NC, own, LANES), F32),
        pltpu.VMEM((UNITS, NYH, NZ, own, LANES), F32),
        pltpu.VMEM(piece, BF16),
        pltpu.VMEM(piece, BF16),
        pltpu.VMEM(piece, BF16),
        pltpu.VMEM((UNITS, NZ - 1, own, LANES), BF16),
        pltpu.VMEM((UNITS, own, LANES), F32),
        pltpu.VMEM((UNITS, NYH, NZ, NC, own, LANES), BF16),
        pltpu.VMEM((UNITS, own, LANES), F32),
        pltpu.VMEM((UNITS, buses, LANES), F32),
        pltpu.VMEM((2, 2, steps, tile, LANES), BF16),
        pltpu.VMEM((2, 2, steps, tile, LANES), BF16),
        pltpu.VMEM(tiles, BF16),
        pltpu.VMEM(tiles, BF16),
        pltpu.VMEM(tiles, BF16),
        pltpu.VMEM(tiles, BF16),
        pltpu.VMEM(tiles[1:], BF16),
        pltpu.VMEM(tiles[1:], BF16),
        pltpu.VMEM(tiles[1:], F32),
        dma,
        dma((UNITS,)),
        dma,
        dma((2, UNITS)),
        dma((2, UNITS)),
        dma((UNITS,)),
        dma((UNITS,)),
        dma((UNITS,)),
        dma((UNITS,)),
        dma((2, UNITS)),
        dma((2, UNITS, 2)),
        dma((2, 2, 2, steps)),
        dma((2, 2, 2 * steps)),
        dma((2, 2, 2 * steps)),
        dma((2, 2 * steps)),
        dma((UNITS,)),
        dma((2 * steps,)),
    ]
    anywhere = pl.BlockSpec(memory_space=pl.ANY)
    return pl.pallas_call(
        kernel,
        out_shape=(
            jax.ShapeDtypeStruct((own, hours), F32),
            jax.ShapeDtypeStruct((buses, LANES), F32),
        ),
        in_specs=[anywhere] * 3,
        out_specs=(anywhere, anywhere),
        scratch_shapes=scratch,
        compiler_params=pltpu.CompilerParams(
            collective_id=0, has_side_effects=True, vmem_limit_bytes=42 * 1024 * 1024
        ),
    )(ptdf, load_codes, limit_codes)


def solution(mesh):
    return jax.shard_map(
        local,
        mesh=mesh,
        in_specs=(P("br", "bus"), P("bus", None), P("br")),
        out_specs=(P(("br", "bus"), None), P("bus", "br")),
        check_vma=False,
    )
```

```python
import jax
import jax.numpy as jnp
from jax import lax
from jax.experimental import pallas as pl
from jax.experimental.pallas import tpu as pltpu
from jax.sharding import PartitionSpec as P

MESH = pl.DeviceIdType.MESH
NX, NYL, NYH, NZ, NC = 4, 2, 2, 8, 2
LANES = 128
UNITS = 8
PARTS = 8
ORDER = (0, 1, 2, 4, 3, 5, 6, 7)
LAGS = (1, 3, 5, 7, 9, 10)
MATMULS = (0, 1, 2, 4)
RELAY_DELAY = (0, 0)
PAIR_DELAY = 1
F32, BF16 = jnp.float32, jnp.bfloat16


def epilogue(flows, limits):
    magnitude = jnp.sqrt(flows * flows + 1.0)
    zvalue = 4.0 * (magnitude / limits - 1.0)
    decay = jnp.exp(-jnp.abs(zvalue))
    penalty = (jnp.maximum(zvalue, 0.0) + jnp.log1p(decay)) * 0.25
    sigmoid = jnp.where(zvalue >= 0.0, 1.0, decay) / (1.0 + decay)
    adjoint = sigmoid * flows / (magnitude * limits)
    return penalty, adjoint


def kernel(
    ptdf, codes, limit_codes, penalty_out, sens_out,
    p_v, codes_v, inj_v, limit_s, limits, part, core_in, y_out, y_in, z_out, z_in, z_own, adj, pen_v, s_v,
    opp_out, opp_in, right_out, left_out, right_in, left_in, pair_out, pair_in,
    p_sem, c_sem, l_sem, core_sem, y_sem, zs_sem, zr_sem, gzs_sem, gzr_sem, gy_sem, gc_sem,
    opp_sem, right_sem, left_sem, pair_sem, pen_sem,
):
    br, bus = lax.axis_index("br"), lax.axis_index("bus")
    x, ylo = lax.rem(br, NX), br // NX
    core, z, yhi = lax.rem(bus, NC), lax.rem(bus // NC, NZ), bus // (NC * NZ)
    rows, buses = p_v.shape
    own = rows // (NYH * NZ * NC)
    steps, tile = opp_out.shape[2], opp_out.shape[3]
    half = steps * tile

    def at_bus(h, zz, c):
        return (br, (h * NZ + zz) * NC + c)

    sibling = at_bus(yhi, z, 1 - core)
    far_y = at_bus(1 - yhi, z, core)

    z_peers = [at_bus(yhi, lax.rem(z + d, NZ), core) for d in range(NZ)]
    right = (ylo * NX + lax.rem(x + 1, NX), bus)
    left = (ylo * NX + lax.rem(x + NX - 1, NX), bus)
    pair = ((1 - ylo) * NX + x, bus)
    partners = [sibling, far_y, right, left, pair] + z_peers[1:]

    def columns(u):
        k, s = u // 2, lax.rem(u, 2)
        ahead = jnp.where(k == 0, 2, jnp.where(k == 1, 1, jnp.where(k == 2, 3, 0)))
        block = lax.rem(x + ahead, NX) + NX * jnp.where(s == 0, 1 - ylo, ylo)
        return pl.ds(pl.multiple_of(block * LANES, LANES), LANES)

    def pick(index, choices):
        value = jnp.int32(choices[-1])
        for i, choice in enumerate(choices[:-1]):
            value = jnp.where(index == i, choice, value)
        return value

    def remote(src, dst, send, recv, device):
        return pltpu.make_async_remote_copy(
            src_ref=src, dst_ref=dst, send_sem=send, recv_sem=recv, device_id=device, device_id_type=MESH
        )

    def codes_copy(u):
        return pltpu.make_async_copy(codes.at[:, columns(u)], codes_v.at[u], c_sem.at[u])

    def p_copy(i):
        at = pl.ds(i * (rows // PARTS), rows // PARTS)
        return pltpu.make_async_copy(ptdf.at[at], p_v.at[at], p_sem.at[i])

    limit_copy = pltpu.make_async_copy(limit_codes, limit_s, l_sem)
    codes_copy(jnp.int32(0)).start()
    codes_copy(jnp.int32(1)).start()
    for i in range(PARTS):
        p_copy(i).start()
    limit_copy.start()
    barrier = pltpu.get_barrier_semaphore()
    for device in partners:
        pl.semaphore_signal(barrier, inc=1, device_id=device, device_id_type=MESH)
    pl.semaphore_wait(barrier, len(partners))

    def core_copy(u):
        return remote(part.at[u, :, :, 1 - core], core_in.at[u], core_sem.at[0, u], core_sem.at[1, u], sibling)

    def y_copy(u):
        return remote(y_out.at[u], y_in.at[u], y_sem.at[0, u], y_sem.at[1, u], far_y)

    def z_copy(u, d):
        return remote(
            z_out.at[u, lax.rem(z + d, NZ)], z_in.at[u, d - 1], zs_sem.at[u], zr_sem.at[u], z_peers[d]
        )

    def gz_copy(u, d):
        mine = adj.at[u, yhi, z, core]
        return remote(mine, mine, gzs_sem.at[u], gzr_sem.at[u], z_peers[d])

    def all_z(u, send, recv):
        return remote(z_in.at[u], z_in.at[u], send.at[u], recv.at[u], z_peers[1])

    def gy_copy(u, h):
        rows_of = adj.at[u, h, :, core]
        return remote(rows_of, rows_of, gy_sem.at[0, u], gy_sem.at[1, u], far_y)

    def gc_copy(u, c):
        rows_of = adj.at[u, :, :, c]
        return remote(rows_of, rows_of, gc_sem.at[0, u], gc_sem.at[1, u], sibling)

    def pen_copy(u):
        return pltpu.make_async_copy(pen_v.at[u], penalty_out.at[:, columns(u)], pen_sem.at[u])

    def stage_matmul(k):
        strip = 256
        for s in range(2):
            codes_copy(2 * k + s).wait()

        def convert(i, _):
            at = pl.ds(pl.multiple_of(i * strip, strip), strip)
            for s in range(2):
                values = codes_v[2 * k + s, at].astype(F32) * (1.0 / 1024.0)
                inj_v[at, s * LANES : (s + 1) * LANES] = values.astype(BF16)
            return 0

        lax.fori_loop(0, buses // strip, convert, 0)
        @pl.when(k == 0)
        def _():
            for i in range(PARTS):
                p_copy(i).wait()
            for u in range(2, UNITS):
                codes_copy(jnp.int32(u)).start()

        product = jnp.dot(p_v[...], inj_v[...], preferred_element_type=F32)
        for s in range(2):
            part[2 * k + s] = product[:, s * LANES : (s + 1) * LANES].reshape(NYH, NZ, NC, own, LANES)

        for s in range(2):
            core_copy(2 * k + s).start()

        @pl.when(k == 0)
        def _():
            limit_copy.wait()
            row = lax.broadcasted_iota(jnp.int32, (own, LANES), 0)
            values = jnp.zeros((own, LANES), F32)
            for i in range(own):
                values = jnp.where(row == i, limit_s[bus * own + i].astype(F32), values)
            limits[...] = values * (1.0 / 64.0)

    def stage_core(u):
        core_copy(u).wait_recv()
        y_out[u] = (part[u, 1 - yhi, :, core] + core_in[u, 1 - yhi]).astype(BF16)
        y_copy(u).start()

    def stage_y(u):
        y_copy(u).wait_recv()
        total = part[u, yhi, :, core] + core_in[u, yhi] + y_in[u].astype(F32)
        part[u, yhi, :, core] = total
        z_out[u] = total.astype(BF16)
        for d in (4, 3, 5, 2, 6, 1, 7):
            z_copy(u, d).start()
        z_own[u] = part[u, yhi, z, core]

    def stage_z(u):
        flows = z_own[u]
        all_z(u, zs_sem, zr_sem).wait_recv()
        for d in range(1, NZ):
            flows = flows + z_in[u, d - 1].astype(F32)
        penalty, adjoint = epilogue(flows, limits[...])
        adj[u, yhi, z, core] = adjoint.astype(BF16)
        for d in (4, 3, 5, 2, 6, 1, 7):
            gz_copy(u, d).start()
        pen_v[u] = penalty
        pen_copy(u).start()

    def stage_gather_z(u):
        all_z(u, gzs_sem, gzr_sem).wait_recv()
        gy_copy(u, yhi).start()

    def stage_gather_y(u):
        gy_copy(u, 1 - yhi).wait_recv()
        gc_copy(u, core).start()

    def opp_copy(s, side, j):
        return remote(
            opp_out.at[s, side, j], opp_in.at[s, side, j], opp_sem.at[0, s, side, j], opp_sem.at[1, s, side, j],
            (right, left)[side],
        )

    def right_copy(s, i):
        return remote(right_out.at[s, i], right_in.at[s, i], right_sem.at[0, s, i], right_sem.at[1, s, i], right)

    def left_copy(s, i):
        return remote(left_out.at[s, i], left_in.at[s, i], left_sem.at[0, s, i], left_sem.at[1, s, i], left)

    def tile_at(i):
        return pl.ds(pl.multiple_of(i * tile, tile), tile)

    def stage_sens(u):
        gc_copy(u, 1 - core).wait_recv()
        k, s = u // 2, lax.rem(u, 2)
        rhs = adj[u].reshape(rows, LANES)
        s_v[u] = lax.dot_general(p_v[...], rhs, (((0,), (0,)), ((), ())), preferred_element_type=F32)

        def opposite(j, _):
            opp_out[s, 0, j] = s_v[u, tile_at(j)].astype(BF16)
            opp_copy(s, 0, j).start()
            opp_out[s, 1, j] = s_v[u, tile_at(steps + j)].astype(BF16)
            opp_copy(s, 1, j).start()
            return 0

        def rightward(j, _):
            right_out[s, steps + j] = s_v[u, tile_at(steps + j)].astype(BF16)
            right_copy(s, steps + j).start()
            return 0

        def leftward(j, _):
            left_out[s, j] = s_v[u, tile_at(j)].astype(BF16)
            left_copy(s, j).start()
            return 0

        for kind, send in enumerate((opposite, rightward, leftward)):

            @pl.when(k == kind)
            def _(send=send):
                lax.fori_loop(0, steps, send, 0)

    def relay(s):
        def body(j, _):
            opp_copy(s, 0, j).wait_recv()
            right_out[s, j] = (s_v[2 + s, tile_at(j)] + opp_in[s, 0, j].astype(F32)).astype(BF16)
            right_copy(s, j).start()
            opp_copy(s, 1, j).wait_recv()
            left_out[s, steps + j] = (s_v[4 + s, tile_at(steps + j)] + opp_in[s, 1, j].astype(F32)).astype(BF16)
            left_copy(s, steps + j).start()
            return 0

        lax.fori_loop(0, steps, body, 0)

    stages = [stage_core, stage_y, stage_z, stage_gather_z, stage_gather_y, stage_sens]
    def pair_copy(i):
        return remote(pair_out.at[i], pair_in.at[i], pair_sem.at[0, i], pair_sem.at[1, i], pair)

    def x_sum(s, i):
        right_copy(s, i).wait_recv()
        left_copy(s, i).wait_recv()
        return s_v[6 + s, tile_at(i)] + right_in[s, i].astype(F32) + left_in[s, i].astype(F32)

    def for_pair(j, _):
        for i in (j, steps + j):
            pair_out[i] = x_sum(0, i).astype(BF16)
            pair_copy(i).start()
        return 0

    def for_self(j, _):
        for i in (j, steps + j):
            total = x_sum(1, i)
            pair_copy(i).wait_recv()
            sens_out[tile_at(i)] = total + pair_in[i].astype(F32)
        return 0

    waits = {unit: ORDER.index(unit) + LAGS[-1] for unit in range(UNITS)}
    relay_at = [max(waits[2 + s], waits[4 + s]) + RELAY_DELAY[s] for s in range(2)]
    pair_at = max(relay_at[0], waits[6]) + PAIR_DELAY

    def run(t, _):
        for lag, stage in reversed(list(zip(LAGS, stages))):
            p = t - lag

            @pl.when((p >= 0) & (p < UNITS))
            def _(p=p, stage=stage):
                stage(pick(p, ORDER))

        this = sum(jnp.where(t == at, k, 0) for k, at in enumerate(MATMULS))

        @pl.when((this > 0) | (t == MATMULS[0]))
        def _():
            stage_matmul(this)

        @pl.when((t == relay_at[0]) | (t == relay_at[1]))
        def _():
            relay(jnp.where(t == relay_at[0], 0, 1))

        @pl.when(t == pair_at)
        def _():
            lax.fori_loop(0, steps, for_pair, 0)

        return 0

    lax.fori_loop(0, max(UNITS + LAGS[-1], relay_at[1] + 1, pair_at + 1), run, 0)
    lax.fori_loop(0, steps, for_self, 0)

    def drain_unit(u, _):
        core_copy(u).wait_send()
        y_copy(u).wait_send()
        gy_copy(u, yhi).wait_send()
        gc_copy(u, core).wait_send()
        all_z(u, zs_sem, zr_sem).wait_send()
        all_z(u, gzs_sem, gzr_sem).wait_send()
        pen_copy(u).wait()
        return 0

    lax.fori_loop(0, UNITS, drain_unit, 0)

    def drain(j, _):
        for side in range(2):
            i = side * steps + j
            for s in range(2):
                opp_copy(s, side, j).wait_send()
                right_copy(s, i).wait_send()
                left_copy(s, i).wait_send()
            pair_copy(i).wait_send()
        return 0

    lax.fori_loop(0, steps, drain, 0)


def local(ptdf, load_codes, limit_codes):
    rows, buses = ptdf.shape
    hours = load_codes.shape[1]
    own = rows // (NYH * NZ * NC)
    tile = 1024
    steps = buses // 2 // tile
    dma = pltpu.SemaphoreType.DMA
    piece = (UNITS, NZ, own, LANES)
    tiles = (2, 2 * steps, tile, LANES)
    scratch = [
        pltpu.VMEM((rows, buses), BF16),
        pltpu.VMEM((UNITS, buses, LANES), jnp.int32),
        pltpu.VMEM((buses, 2 * LANES), BF16),
        pltpu.SMEM((rows,), jnp.int32),
        pltpu.VMEM((own, LANES), F32),
        pltpu.VMEM((UNITS, NYH, NZ, NC, own, LANES), F32),
        pltpu.VMEM((UNITS, NYH, NZ, own, LANES), F32),
        pltpu.VMEM(piece, BF16),
        pltpu.VMEM(piece, BF16),
        pltpu.VMEM(piece, BF16),
        pltpu.VMEM((UNITS, NZ - 1, own, LANES), BF16),
        pltpu.VMEM((UNITS, own, LANES), F32),
        pltpu.VMEM((UNITS, NYH, NZ, NC, own, LANES), BF16),
        pltpu.VMEM((UNITS, own, LANES), F32),
        pltpu.VMEM((UNITS, buses, LANES), F32),
        pltpu.VMEM((2, 2, steps, tile, LANES), BF16),
        pltpu.VMEM((2, 2, steps, tile, LANES), BF16),
        pltpu.VMEM(tiles, BF16),
        pltpu.VMEM(tiles, BF16),
        pltpu.VMEM(tiles, BF16),
        pltpu.VMEM(tiles, BF16),
        pltpu.VMEM(tiles[1:], BF16),
        pltpu.VMEM(tiles[1:], BF16),
        dma((PARTS,)),
        dma((UNITS,)),
        dma,
        dma((2, UNITS)),
        dma((2, UNITS)),
        dma((UNITS,)),
        dma((UNITS,)),
        dma((UNITS,)),
        dma((UNITS,)),
        dma((2, UNITS)),
        dma((2, UNITS)),
        dma((2, 2, 2, steps)),
        dma((2, 2, 2 * steps)),
        dma((2, 2, 2 * steps)),
        dma((2, 2 * steps)),
        dma((UNITS,)),
    ]
    anywhere = pl.BlockSpec(memory_space=pl.ANY)
    return pl.pallas_call(
        kernel,
        out_shape=(
            jax.ShapeDtypeStruct((own, hours), F32),
            jax.ShapeDtypeStruct((buses, LANES), F32),
        ),
        in_specs=[anywhere] * 3,
        out_specs=(anywhere, pl.BlockSpec(memory_space=pltpu.VMEM)),
        scratch_shapes=scratch,
        compiler_params=pltpu.CompilerParams(
            collective_id=0, has_side_effects=True, vmem_limit_bytes=42 * 1024 * 1024
        ),
    )(ptdf, load_codes, limit_codes)


def solution(mesh):
    return jax.shard_map(
        local,
        mesh=mesh,
        in_specs=(P("br", "bus"), P("bus", None), P("br")),
        out_specs=(P(("br", "bus"), None), P("bus", "br")),
        check_vma=False,
    )
```
